32 devices in a mesh: hier: 8 (over y, x, core), col: 4 (over z).
Axes of the slice: x: 2, y: 2, z: 4, core: 2. Of those that a mesh axis runs over, the one named last changes fastest.
Arguments:
- densities: float32 [32, 2, 256, 256], P('hier', None, 'col'), may hold values from -6 to 6
- hamiltonian: float32 [256, 256], replicated, may hold values from -0.35355339 to 0.35355339, as said below
- couplings: float32 [2, 256, 256], replicated, may hold values from -0.088388348 to 0.088388348, as said below
- gamma: float32 [2], replicated, may hold values from 0.005 to 0.05
- coeff: float32 [2, 2], replicated, may hold values from -0.5 to 0.5
- node_count: int32 [8], replicated, may hold values from 2 to 4, as said below
Outputs:
- new_densities: float32 [32, 2, 256, 256], P('hier', None, 'col')
The draws below stay inside these ranges and needn't reach their ends.
Inputs may be any that keep to these rules, and one draw needn't show every extreme that they name: `node_count`: at least one index of hier holds 4 nodes; every index holds 2 or more. `hamiltonian`: symmetric. `couplings`: each of the two matrices is symmetric.
All inputs are finite; a program needn't handle non-finite values.
Results may differ from the reference program's by a relative error of at most 0.00012.
Values sent between devices are 32-bit elements; how exact they have to be, the bound alone decides.
A program may use at most 64 MiB of HBM per device.

```python
import math
import jax
import jax.numpy as jnp
from jax import lax

D = 256
NODE_DEV = 4
DEPTH2 = 2
SHARDS = 8
SLOTS = 32


def draw_hamiltonian(key, part):
    base = jax.random.truncated_normal(key, -4.0, 4.0, (D, D), jnp.float32)
    return ((base + base.T) / jnp.sqrt(2.0 * D)).astype(jnp.float32)


def draw_couplings(key, part):
    base = jax.random.truncated_normal(jax.random.fold_in(key, 7), -4.0, 4.0, (2, D, D), jnp.float32)
    return (0.25 * (base + jnp.swapaxes(base, 1, 2)) / jnp.sqrt(2.0 * D)).astype(jnp.float32)


def draw_node_count(key, part):
    key_counts, key_full = jax.random.split(jax.random.fold_in(key, 11))
    counts = jax.random.randint(key_counts, (SHARDS,), NODE_DEV // 2, NODE_DEV + 1)
    full_index = jax.random.randint(key_full, (), 0, SHARDS)
    return jnp.where(jnp.arange(SHARDS) == full_index, NODE_DEV, counts).astype(jnp.int32)


def steps_of(rng, extent, cuts, smallest, largest):
    level = 1.0
    for axis_at, blocks in cuts:
        draws = jax.random.uniform(jax.random.fold_in(jax.random.fold_in(rng, 6), axis_at), (blocks,), jnp.float32, smallest / len(cuts), largest / len(cuts))
        level = level * jnp.repeat(jnp.exp(draws), extent[axis_at] // blocks).reshape((-1,) + (1,) * (len(extent) - 1 - axis_at))
    return level


def normal_values(stream_key, extent, width, limit, cuts=(), held_as=jnp.bfloat16):
    loudness = steps_of(stream_key, extent, cuts, -0.22, 0.18) if cuts else 1.0
    entries = jax.random.normal(stream_key, extent, jnp.float32) * width * loudness
    return jnp.minimum(jnp.maximum(entries, -limit), limit).astype(held_as)


def setup_inputs(seed: int = 0) -> dict:
    seeds = jax.random.split(jax.random.key(seed), 7)
    return {
        "densities": normal_values(seeds[0], (SLOTS, 2, D, D), 1.0, 6.0, ((0, 8), (2, 4)), jnp.float32),
        "hamiltonian": draw_hamiltonian(jax.random.fold_in(seeds[6], 71), 0),
        "couplings": draw_couplings(jax.random.fold_in(seeds[6], 71), 0),
        "gamma": jnp.clip(jnp.exp(jax.random.uniform(seeds[3], (2,), jnp.float32, math.log(0.005), math.log(0.05))), 0.005, 0.05),
        "coeff": jnp.clip(jax.random.uniform(seeds[4], (2, 2), jnp.float32, -0.5, 0.5), -0.5, 0.5),
        "node_count": draw_node_count(jax.random.fold_in(seeds[6], 71), 0),
    }


step_size = 0.2

def hierarchy(node_count, device, slot):
    shards = node_count.shape[0]
    columns = jnp.arange(shards, dtype=jnp.int32)
    counts = node_count.astype(jnp.int32)
    offsets = (jnp.cumsum(counts) - counts).astype(jnp.int32)
    live_total = (jnp.sum(counts).astype(jnp.int32) // DEPTH2 * DEPTH2).astype(jnp.int32)

    def lookup(table, which):
        return lax.optimization_barrier(jnp.sum(jnp.where(which[:, None] == columns[None, :], table[None, :], 0), axis=1)).astype(jnp.int32)
    index = (lookup(offsets, device) + slot).astype(jnp.int32)
    live = (slot < lookup(counts, device)) & (index < live_total)
    first = index // DEPTH2
    second = index % DEPTH2
    targets = (index + DEPTH2, index + 1, index - DEPTH2, index - 1)
    allowed = (live & (index + DEPTH2 < live_total), live & (second + 1 < DEPTH2), live & (first > 0), live & (second > 0))
    found = []
    for target, valid in zip(targets, allowed):
        owner = (lax.optimization_barrier(jnp.sum((offsets[None, :] <= target[:, None]).astype(jnp.int32), axis=1)) - 1).astype(jnp.int32)
        within = (target - lookup(offsets, owner)).astype(jnp.int32)
        found.append((owner, within, valid))
    return (live, first, second, found)

def combine(upward, downward, raise_w, lower_w, real, imag):
    rise = raise_w[:, None, None]
    fall = lower_w[:, None, None]
    part_re = rise * upward[:, 0] + fall * (real * downward[:, 0] - imag * downward[:, 1])
    part_im = rise * upward[:, 1] + fall * (real * downward[:, 1] + imag * downward[:, 0])
    return jnp.stack([part_re, part_im], axis=1)

def mixes(linked, levels, coeff, sign):
    result = []
    for mode in range(2):
        result.append(combine(linked[mode], linked[mode + 2], jnp.sqrt(levels[mode] + 1.0), jnp.sqrt(levels[mode]), coeff[mode, 0], sign * coeff[mode, 1]))
    return result

def reference(densities, hamiltonian, couplings, gamma, coeff, node_count):
    device = jnp.repeat(jnp.arange(SHARDS, dtype=jnp.int32), NODE_DEV)
    slot = jnp.tile(jnp.arange(NODE_DEV, dtype=jnp.int32), SHARDS)
    live, first, second, found = hierarchy(node_count, device, slot)
    positions = jnp.stack([jnp.where(v, o * NODE_DEV + w, 0).astype(jnp.int32) for o, w, v in found], axis=1)
    valid = jnp.stack([v.astype(jnp.float32) for o, w, v in found], axis=1)
    levels = jnp.stack([first.astype(jnp.float32), second.astype(jnp.float32)], axis=1)
    alive = live.astype(jnp.float32)
    left_mat = jnp.concatenate([hamiltonian, couplings[0], couplings[1]], axis=1)
    right_mat = jnp.concatenate([hamiltonian, couplings[0], couplings[1]], axis=0)
    high = lax.Precision.HIGHEST

    def slope(state):

        def one(block):
            own, pos, val, lev, keep = block
            linked = [jnp.take(state, pos[:, j], axis=0) * val[:, j][:, None, None, None] for j in range(4)]
            lev_pair = (lev[:, 0], lev[:, 1])
            lefts = mixes(linked, lev_pair, coeff, 1.0)
            rights = mixes(linked, lev_pair, coeff, -1.0)
            left = jnp.einsum('ij,scjk->scik', left_mat, jnp.concatenate([own] + lefts, axis=2), precision=high)
            right = jnp.einsum('scij,jk->scik', jnp.concatenate([own] + rights, axis=3), right_mat, precision=high)
            comm = left - right
            damping = (lev[:, 0] * gamma[0] + lev[:, 1] * gamma[1])[:, None, None]
            out_re = comm[:, 1] - damping * own[:, 0]
            out_im = -comm[:, 0] - damping * own[:, 1]
            return jnp.stack([out_re, out_im], axis=1) * keep[:, None, None, None]
        blocks = (state.reshape(SHARDS, NODE_DEV, 2, D, D), positions.reshape(SHARDS, NODE_DEV, 4), valid.reshape(SHARDS, NODE_DEV, 4), levels.reshape(SHARDS, NODE_DEV, 2), alive.reshape(SHARDS, NODE_DEV))
        return lax.map(one, blocks).reshape(SLOTS, 2, D, D)
    first_slope = slope(densities)
    middle = densities + 0.5 * step_size * first_slope
    second_slope = slope(middle)
    return densities + step_size * second_slope
```

```python
import functools

import jax
import jax.numpy as jnp
from jax import lax
from jax.experimental import pallas as pl
from jax.experimental.pallas import tpu as pltpu
from jax.sharding import PartitionSpec as P

DEPTH2 = 2
MESH = pl.DeviceIdType.MESH
step_size = 0.2


def split(value):
    high = value.astype(jnp.bfloat16)
    low = (value - high.astype(jnp.float32)).astype(jnp.bfloat16)
    return high, low


def product(both, high, rhs_high, rhs_low):
    rows = high.shape[0]
    wide = jnp.dot(both, rhs_high, preferred_element_type=jnp.float32)
    rest = jnp.dot(high, rhs_low, preferred_element_type=jnp.float32)
    return wide[:rows] + (wide[rows:] + rest)


def kernel(
    shards,
    ring,
    counts,
    gamma,
    coeff,
    x_ref,
    h_ref,
    q_ref,
    out_ref,
    full,
    mid,
    right_high,
    right_low,
    left_both,
    lefts,
    rights,
    to_upper,
    to_lower,
    from_lower,
    from_upper,
    ring_send,
    ring_recv,
    hop_send,
    hop_recv,
    own_sem,
):
    slots, _, rows, order = x_ref.shape
    here = lax.axis_index("hier")
    me = lax.axis_index("col")
    reach = ring // 2
    right = (here, lax.rem(me + 1, ring))
    left = (here, lax.rem(me + ring - 1, ring))
    has_lower = here > 0
    has_upper = here < shards - 1

    barrier = pltpu.get_barrier_semaphore()
    for neighbour in (left, right):
        pl.semaphore_signal(barrier, inc=1, device_id=neighbour, device_id_type=MESH)

    @pl.when(has_lower)
    def _():
        pl.semaphore_signal(barrier, inc=1, device_id=(here - 1, me), device_id_type=MESH)

    @pl.when(has_upper)
    def _():
        pl.semaphore_signal(barrier, inc=1, device_id=(here + 1, me), device_id_type=MESH)

    pl.semaphore_wait(barrier, 2 + has_lower.astype(jnp.int32) + has_upper.astype(jnp.int32))

    def panel(origin):
        return pl.ds(pl.multiple_of(lax.rem(origin + ring, ring) * rows, rows), rows)

    def ring_copy(section, way, distance, s, origin):
        first, size = (way, 1) if 2 * distance == ring else (0, 2)
        parts = pl.ds(first, size)
        place = full.at[section, s, parts, panel(origin), :]
        if distance == 1:
            source = (x_ref if section == 0 else mid).at[s, parts]
        else:
            source = place
        return pltpu.make_async_remote_copy(
            src_ref=source,
            dst_ref=place,
            send_sem=ring_send.at[section, way, distance - 1, s],
            recv_sem=ring_recv.at[section, way, distance - 1, s],
            device_id=right if way == 0 else left,
            device_id_type=MESH,
        )

    def sent(section, way, distance, s):
        origin = me - (distance - 1) if way == 0 else me + (distance - 1)
        return ring_copy(section, way, distance, s, origin)

    def arrived(section, way, distance, s):
        origin = me - distance if way == 0 else me + distance
        return ring_copy(section, way, distance, s, origin)

    def own_copy(section, s):
        source = (x_ref if section == 0 else mid).at[s]
        return pltpu.make_async_copy(
            source, full.at[section, s, :, panel(me), :], own_sem.at[section, s]
        )

    def hop_copy(section, way):
        source, place = (to_upper, from_lower) if way == 0 else (to_lower, from_upper)
        return pltpu.make_async_remote_copy(
            src_ref=source.at[section],
            dst_ref=place.at[section],
            send_sem=hop_send.at[section, way],
            recv_sem=hop_recv.at[section, way],
            device_id=(here + 1, me) if way == 0 else (here - 1, me),
            device_id_type=MESH,
        )

    def start_slot(section, s):
        for way in range(2):
            sent(section, way, 1, s).start()
        own_copy(section, s).start()

    for s in range(slots):
        start_slot(0, s)

    for section in range(2):

        @pl.when(jnp.logical_not(has_lower))
        def _():
            from_lower[section] = jnp.zeros(from_lower.shape[1:], jnp.float32)

        @pl.when(jnp.logical_not(has_upper))
        def _():
            from_upper[section] = jnp.zeros(from_upper.shape[1:], jnp.float32)

    mine = panel(me)
    for a in range(3):
        high, low = split(h_ref[...] if a == 0 else q_ref[a - 1])
        right_high[a], right_low[a] = high, low
        high, low = split(h_ref[mine, :] if a == 0 else q_ref[a - 1, mine, :])
        left_both[a * rows : (a + 1) * rows] = high
        left_both[(3 + a) * rows : (4 + a) * rows] = low

    offset = jnp.int32(0)
    total = jnp.int32(0)
    count = jnp.int32(0)
    for i in range(shards):
        held = counts[i]
        total = total + held
        offset = offset + jnp.where(here > i, held, 0)
        count = count + jnp.where(here == i, held, 0)
    live_total = total // DEPTH2 * DEPTH2

    def number(flag):
        return jnp.where(flag, jnp.float32(1), jnp.float32(0))

    def root(value):
        return jnp.sqrt(jnp.full((1, order), value, jnp.float32))

    def levels(q):
        node = offset + q
        level = (node + DEPTH2) // DEPTH2 - 1
        return level, node - level * DEPTH2, (node >= 0) & (node < live_total)

    alive, damping = [], []
    for s in range(slots):
        zeroth, first, inside = levels(s)
        alive.append(number(inside & (s < count)))
        damping.append(
            zeroth.astype(jnp.float32) * gamma[0] + first.astype(jnp.float32) * gamma[1]
        )
    edges = range(-DEPTH2, slots + DEPTH2)
    weights = {}
    for q in edges:
        zeroth, first, inside = levels(q)
        target = number(inside)
        base = jnp.maximum(zeroth, 0).astype(jnp.float32)
        above = first.astype(jnp.float32)
        if 0 <= q + DEPTH2 < slots:
            weights[q, "up0"] = root(base + 1.0) * (target * alive[q + DEPTH2])
        if 0 <= q - DEPTH2 < slots:
            weights[q, "down0"] = root(base) * (target * alive[q - DEPTH2])
        if 0 <= q + 1 < slots:
            ok = number(first + 1 < DEPTH2)
            weights[q, "up1"] = root(above + 1.0) * (target * alive[q + 1] * ok)
        if 0 <= q - 1 < slots:
            weights[q, "down1"] = root(above) * (target * alive[q - 1])

    def gathered(q):
        total_re = total_im = None

        def plus(total, term):
            return term if total is None else total + term

        for mode, stride in ((0, DEPTH2), (1, 1)):
            a = mode + 1
            for name, m in (("up", q + stride), ("down", q - stride)):
                if not 0 <= m < slots:
                    continue
                weight = weights[q, f"{name}{mode}"]
                left_re = lefts[m, 0, a * rows : (a + 1) * rows]
                left_im = lefts[m, 1, a * rows : (a + 1) * rows]
                right_re, right_im = rights[m, 0, a], rights[m, 1, a]
                if name == "up":
                    total_re = plus(total_re, weight * (left_re - right_re))
                    total_im = plus(total_im, weight * (left_im - right_im))
                else:
                    real = weight * coeff[mode, 0]
                    imag = weight * coeff[mode, 1]
                    total_re = plus(
                        total_re, real * (left_re - right_re) - imag * (left_im + right_im)
                    )
                    total_im = plus(
                        total_im, real * (left_im - right_im) + imag * (left_re + right_re)
                    )
        return total_re, total_im

    for section in range(2):
        state = x_ref if section == 0 else mid

        high, low = split(state[...].reshape(slots * 2 * rows, order))
        both = jnp.concatenate([high, low], axis=0)
        for a in range(3):
            value = product(both, high, right_high[a], right_low[a])
            rights[:, :, a] = value.reshape(slots, 2, rows, order)

        for distance in range(1, reach + 1):
            for s in range(slots):
                for way in range(2):
                    if 2 * (distance + 1) > ring + (ring % 2 == 1):
                        continue
                    arrived(section, way, distance, s).wait_recv()
                for way in range(2):
                    if 2 * (distance + 1) > ring + (ring % 2 == 1):
                        continue
                    sent(section, way, distance + 1, s).start()

        left_high = left_both[: 3 * rows]
        for s in range(slots):
            own_copy(section, s).wait()
            for way in range(2):
                arrived(section, way, reach, s).wait_recv()
            for p in range(2):
                high, low = split(full[section, s, p])
                lefts[s, p] = product(left_both[...], left_high, high, low)

        near = {}
        for q in edges:
            if q < 0:
                low_re, low_im = gathered(q)
                to_lower[section, q + DEPTH2, 0] = low_re
                to_lower[section, q + DEPTH2, 1] = low_im
            else:
                near[q] = gathered(q)
        for j in range(DEPTH2):
            for p in range(2):
                value = None
                for q in range(DEPTH2 + j, slots + j + 1):
                    term = number(count + j == q) * near[q][p]
                    value = term if value is None else value + term
                to_upper[section, j, p] = value

        @pl.when(has_lower)
        def _():
            hop_copy(section, 1).start()

        @pl.when(has_upper)
        def _():
            hop_copy(section, 0).start()

        @pl.when(has_lower)
        def _():
            hop_copy(section, 0).wait_recv()

        @pl.when(has_upper)
        def _():
            hop_copy(section, 1).wait_recv()

        for s in range(slots):
            parts = []
            for p in range(2):
                value = lefts[s, p, :rows] - rights[s, p, 0] + near[s][p]
                if s < DEPTH2:
                    value = value + from_lower[section, s, p]
                for j in range(DEPTH2):
                    value = value + number(s == count - DEPTH2 + j) * from_upper[section, j, p]
                parts.append(value)
            keep = alive[s]
            slope_re = (parts[1] - damping[s] * state[s, 0]) * keep
            slope_im = (-parts[0] - damping[s] * state[s, 1]) * keep
            if section == 0:
                mid[s, 0] = x_ref[s, 0] + 0.5 * step_size * slope_re
                mid[s, 1] = x_ref[s, 1] + 0.5 * step_size * slope_im
                start_slot(1, s)
            else:
                out_ref[s, 0] = x_ref[s, 0] + step_size * slope_re
                out_ref[s, 1] = x_ref[s, 1] + step_size * slope_im

    for section in range(2):
        for s in range(slots):
            for distance in range(1, reach + 1):
                for way in range(2):
                    sent(section, way, distance, s).wait_send()

        @pl.when(has_lower)
        def _():
            hop_copy(section, 1).wait_send()

        @pl.when(has_upper)
        def _():
            hop_copy(section, 0).wait_send()


def solution(mesh):
    shards, ring = mesh.shape["hier"], mesh.shape["col"]

    def on_device(densities, hamiltonian, couplings, gamma, coeff, node_count):
        slots, _, rows, order = densities.shape
        f32, bf16 = jnp.float32, jnp.bfloat16
        vmem = pl.BlockSpec(memory_space=pltpu.VMEM)
        smem = pl.BlockSpec(memory_space=pltpu.SMEM)
        edge = (2, DEPTH2, 2, rows, order)
        dma = pltpu.SemaphoreType.DMA
        return pl.pallas_call(
            functools.partial(kernel, shards, ring),
            out_shape=jax.ShapeDtypeStruct(densities.shape, f32),
            in_specs=[smem] * 3 + [vmem] * 3,
            out_specs=vmem,
            scratch_shapes=[
                pltpu.VMEM((2, slots, 2, order, order), f32),
                pltpu.VMEM((slots, 2, rows, order), f32),
                pltpu.VMEM((3, order, order), bf16),
                pltpu.VMEM((3, order, order), bf16),
                pltpu.VMEM((6 * rows, order), bf16),
                pltpu.VMEM((slots, 2, 3 * rows, order), f32),
                pltpu.VMEM((slots, 2, 3, rows, order), f32),
                pltpu.VMEM(edge, f32),
                pltpu.VMEM(edge, f32),
                pltpu.VMEM(edge, f32),
                pltpu.VMEM(edge, f32),
                dma((2, 2, ring // 2, slots)),
                dma((2, 2, ring // 2, slots)),
                dma((2, 2)),
                dma((2, 2)),
                dma((2, slots)),
            ],
            compiler_params=pltpu.CompilerParams(
                collective_id=0, has_side_effects=True, vmem_limit_bytes=50 * 1024 * 1024
            ),
        )(node_count, gamma, coeff, densities, hamiltonian, couplings)

    return jax.shard_map(
        on_device,
        mesh=mesh,
        in_specs=(P("hier", None, "col", None), P(), P(), P(), P(), P()),
        out_specs=P("hier", None, "col", None),
        check_vma=False,
    )
```

```python
import functools

import jax
import jax.numpy as jnp
from jax import lax
from jax.experimental import pallas as pl
from jax.experimental.pallas import tpu as pltpu
from jax.sharding import PartitionSpec as P

DEPTH2 = 2
MESH = pl.DeviceIdType.MESH
step_size = 0.2


def split(value):
    high = value.astype(jnp.bfloat16)
    low = (value - high.astype(jnp.float32)).astype(jnp.bfloat16)
    return high, low


def product(both, high, rhs_high, rhs_low):
    rows = high.shape[0]
    wide = jnp.dot(both, rhs_high, preferred_element_type=jnp.float32)
    rest = jnp.dot(high, rhs_low, preferred_element_type=jnp.float32)
    return wide[:rows] + (wide[rows:] + rest)


def kernel(
    shards,
    ring,
    counts,
    gamma,
    coeff,
    x_hbm,
    h_hbm,
    q_hbm,
    out_ref,
    x_ref,
    h_ref,
    q_ref,
    full,
    mid,
    right_high,
    right_low,
    left_both,
    lefts,
    rights,
    to_upper,
    to_lower,
    from_lower,
    from_upper,
    ring_send,
    ring_recv,
    hop_send,
    hop_recv,
    own_sem,
    load_sem,
):
    slots, _, rows, order = x_hbm.shape
    here = lax.axis_index("hier")
    me = lax.axis_index("col")
    reach = ring // 2
    right = (here, lax.rem(me + 1, ring))
    left = (here, lax.rem(me + ring - 1, ring))
    has_lower = here > 0
    has_upper = here < shards - 1

    loads = [
        pltpu.make_async_copy(source, place, load_sem.at[i])
        for i, (source, place) in enumerate(((x_hbm, x_ref), (h_hbm, h_ref), (q_hbm, q_ref)))
    ]
    for load in loads:
        load.start()

    barrier = pltpu.get_barrier_semaphore()
    for neighbour in (left, right):
        pl.semaphore_signal(barrier, inc=1, device_id=neighbour, device_id_type=MESH)

    @pl.when(has_lower)
    def _():
        pl.semaphore_signal(barrier, inc=1, device_id=(here - 1, me), device_id_type=MESH)

    @pl.when(has_upper)
    def _():
        pl.semaphore_signal(barrier, inc=1, device_id=(here + 1, me), device_id_type=MESH)

    pl.semaphore_wait(barrier, 2 + has_lower.astype(jnp.int32) + has_upper.astype(jnp.int32))

    def panel(origin):
        return pl.ds(pl.multiple_of(lax.rem(origin + ring, ring) * rows, rows), rows)

    def ring_copy(section, way, distance, s, origin):
        first, size = (way, 1) if 2 * distance == ring else (0, 2)
        parts = pl.ds(first, size)
        place = full.at[section, s, parts, panel(origin), :]
        if distance == 1:
            source = (x_hbm if section == 0 else mid).at[s, parts]
        else:
            source = place
        return pltpu.make_async_remote_copy(
            src_ref=source,
            dst_ref=place,
            send_sem=ring_send.at[section, way, distance - 1, s],
            recv_sem=ring_recv.at[section, way, distance - 1, s],
            device_id=right if way == 0 else left,
            device_id_type=MESH,
        )

    def sent(section, way, distance, s):
        origin = me - (distance - 1) if way == 0 else me + (distance - 1)
        return ring_copy(section, way, distance, s, origin)

    def arrived(section, way, distance, s):
        origin = me - distance if way == 0 else me + distance
        return ring_copy(section, way, distance, s, origin)

    def own_copy(section, s):
        source = (x_hbm if section == 0 else mid).at[s]
        return pltpu.make_async_copy(
            source, full.at[section, s, :, panel(me), :], own_sem.at[section, s]
        )

    def hop_copy(section, way):
        source, place = (to_upper, from_lower) if way == 0 else (to_lower, from_upper)
        return pltpu.make_async_remote_copy(
            src_ref=source.at[section],
            dst_ref=place.at[section],
            send_sem=hop_send.at[section, way],
            recv_sem=hop_recv.at[section, way],
            device_id=(here + 1, me) if way == 0 else (here - 1, me),
            device_id_type=MESH,
        )

    def start_slot(section, s):
        for way in range(2):
            sent(section, way, 1, s).start()
        own_copy(section, s).start()

    early, late = range(DEPTH2), range(DEPTH2, slots)
    for s in early:
        start_slot(0, s)

    for section in range(2):

        @pl.when(jnp.logical_not(has_lower))
        def _():
            from_lower[section] = jnp.zeros(from_lower.shape[1:], jnp.float32)

        @pl.when(jnp.logical_not(has_upper))
        def _():
            from_upper[section] = jnp.zeros(from_upper.shape[1:], jnp.float32)

    for load in loads:
        load.wait()
    mine = panel(me)
    for a in range(3):
        high, low = split(h_ref[...] if a == 0 else q_ref[a - 1])
        right_high[a], right_low[a] = high, low
        high, low = split(h_ref[mine, :] if a == 0 else q_ref[a - 1, mine, :])
        left_both[a * rows : (a + 1) * rows] = high
        left_both[(3 + a) * rows : (4 + a) * rows] = low

    offset = jnp.int32(0)
    total = jnp.int32(0)
    count = jnp.int32(0)
    for i in range(shards):
        held = counts[i]
        total = total + held
        offset = offset + jnp.where(here > i, held, 0)
        count = count + jnp.where(here == i, held, 0)
    live_total = total // DEPTH2 * DEPTH2

    def number(flag):
        return jnp.where(flag, jnp.float32(1), jnp.float32(0))

    def root(value):
        return jnp.sqrt(jnp.full((1, order), value, jnp.float32))

    def levels(q):
        node = offset + q
        level = (node + DEPTH2) // DEPTH2 - 1
        return level, node - level * DEPTH2, (node >= 0) & (node < live_total)

    alive, damping = [], []
    for s in range(slots):
        zeroth, first, inside = levels(s)
        alive.append(number(inside & (s < count)))
        damping.append(
            zeroth.astype(jnp.float32) * gamma[0] + first.astype(jnp.float32) * gamma[1]
        )
    edges = range(-DEPTH2, slots + DEPTH2)
    weights = {}
    for q in edges:
        zeroth, first, inside = levels(q)
        target = number(inside)
        base = jnp.maximum(zeroth, 0).astype(jnp.float32)
        above = first.astype(jnp.float32)
        if 0 <= q + DEPTH2 < slots:
            weights[q, "up0"] = root(base + 1.0) * (target * alive[q + DEPTH2])
        if 0 <= q - DEPTH2 < slots:
            weights[q, "down0"] = root(base) * (target * alive[q - DEPTH2])
        if 0 <= q + 1 < slots:
            ok = number(first + 1 < DEPTH2)
            weights[q, "up1"] = root(above + 1.0) * (target * alive[q + 1] * ok)
        if 0 <= q - 1 < slots:
            weights[q, "down1"] = root(above) * (target * alive[q - 1])

    def gathered(q):
        total_re = total_im = None

        def plus(total, term):
            return term if total is None else total + term

        for mode, stride in ((0, DEPTH2), (1, 1)):
            a = mode + 1
            for name, m in (("up", q + stride), ("down", q - stride)):
                if not 0 <= m < slots:
                    continue
                weight = weights[q, f"{name}{mode}"]
                left_re = lefts[m, 0, a * rows : (a + 1) * rows]
                left_im = lefts[m, 1, a * rows : (a + 1) * rows]
                right_re, right_im = rights[m, 0, a], rights[m, 1, a]
                if name == "up":
                    total_re = plus(total_re, weight * (left_re - right_re))
                    total_im = plus(total_im, weight * (left_im - right_im))
                else:
                    real = weight * coeff[mode, 0]
                    imag = weight * coeff[mode, 1]
                    total_re = plus(
                        total_re, real * (left_re - right_re) - imag * (left_im + right_im)
                    )
                    total_im = plus(
                        total_im, real * (left_im - right_im) + imag * (left_re + right_re)
                    )
        return total_re, total_im

    left_high = left_both[: 3 * rows]

    def right_products(section, chosen):
        state = x_ref if section == 0 else mid
        first, size = chosen[0], len(chosen)
        value = state[first : first + size].reshape(size * 2 * rows, order)
        high, low = split(value)
        both = jnp.concatenate([high, low], axis=0)
        for a in range(3):
            value = product(both, high, right_high[a], right_low[a])
            rights[first : first + size, :, a] = value.reshape(size, 2, rows, order)

    def forward(section, s):
        for distance in range(1, reach):
            for way in range(2):
                arrived(section, way, distance, s).wait_recv()
            for way in range(2):
                sent(section, way, distance + 1, s).start()

    def finish(section, s):
        own_copy(section, s).wait()
        for way in range(2):
            arrived(section, way, reach, s).wait_recv()
        for p in range(2):
            high, low = split(full[section, s, p])
            lefts[s, p] = product(left_both[...], left_high, high, low)

    def send_lower(section):
        for q in range(-DEPTH2, 0):
            value = gathered(q)
            for p in range(2):
                to_lower[section, q + DEPTH2, p] = value[p]

        @pl.when(has_lower)
        def _():
            hop_copy(section, 1).start()

    def send_upper(section, near):
        for j in range(DEPTH2):
            for p in range(2):
                value = None
                for q in range(DEPTH2 + j, slots + j + 1):
                    term = number(count + j == q) * near[q][p]
                    value = term if value is None else value + term
                to_upper[section, j, p] = value

        @pl.when(has_upper)
        def _():
            hop_copy(section, 0).start()

    def wait_upper(section):
        @pl.when(has_upper)
        def _():
            hop_copy(section, 1).wait_recv()

    def wait_lower(section):
        @pl.when(has_lower)
        def _():
            hop_copy(section, 0).wait_recv()

    def update(section, s, near):
        state = x_ref if section == 0 else mid
        parts = []
        for p in range(2):
            value = lefts[s, p, :rows] - rights[s, p, 0] + near[s][p]
            if s < DEPTH2:
                value = value + from_lower[section, s, p]
            for j in range(DEPTH2):
                value = value + number(s == count - DEPTH2 + j) * from_upper[section, j, p]
            parts.append(value)
        slope_re = (parts[1] - damping[s] * state[s, 0]) * alive[s]
        slope_im = (-parts[0] - damping[s] * state[s, 1]) * alive[s]
        place, length = (mid, 0.5 * step_size) if section == 0 else (out_ref, step_size)
        place[s, 0] = x_ref[s, 0] + length * slope_re
        place[s, 1] = x_ref[s, 1] + length * slope_im

    right_products(0, range(slots))
    for i, s in enumerate(early):
        forward(0, s)
        if DEPTH2 + i < slots:
            start_slot(0, DEPTH2 + i)
    for s in range(slots):
        if s >= 1 and s + DEPTH2 - 1 < slots:
            forward(0, s + DEPTH2 - 1)
        if s == DEPTH2:
            send_lower(0)
        finish(0, s)
    near = {q: gathered(q) for q in range(DEPTH2, slots + DEPTH2)}
    send_upper(0, near)
    wait_upper(0)
    for s in late:
        update(0, s, near)
        start_slot(1, s)
    near = {q: gathered(q) for q in early}
    for s in late:
        forward(1, s)
    wait_lower(0)
    for s in early:
        update(0, s, near)
        start_slot(1, s)
    right_products(1, early)
    right_products(1, late)
    for s in late:
        finish(1, s)
    for s in early:
        forward(1, s)
    for s in early:
        finish(1, s)
    send_lower(1)
    near = {q: gathered(q) for q in range(DEPTH2, slots + DEPTH2)}
    send_upper(1, near)
    near.update({q: gathered(q) for q in early})
    wait_upper(1)
    wait_lower(1)
    for s in range(slots):
        update(1, s, near)

    for section in range(2):
        for s in range(slots):
            for distance in range(1, reach + 1):
                for way in range(2):
                    sent(section, way, distance, s).wait_send()

        @pl.when(has_lower)
        def _():
            hop_copy(section, 1).wait_send()

        @pl.when(has_upper)
        def _():
            hop_copy(section, 0).wait_send()


def solution(mesh):
    shards, ring = mesh.shape["hier"], mesh.shape["col"]

    def on_device(densities, hamiltonian, couplings, gamma, coeff, node_count):
        slots, _, rows, order = densities.shape
        f32, bf16 = jnp.float32, jnp.bfloat16
        vmem = pl.BlockSpec(memory_space=pltpu.VMEM)
        smem = pl.BlockSpec(memory_space=pltpu.SMEM)
        edge = (2, DEPTH2, 2, rows, order)
        dma = pltpu.SemaphoreType.DMA
        return pl.pallas_call(
            functools.partial(kernel, shards, ring),
            out_shape=jax.ShapeDtypeStruct(densities.shape, f32),
            in_specs=[smem] * 3 + [pl.BlockSpec(memory_space=pltpu.HBM)] * 3,
            out_specs=vmem,
            scratch_shapes=[
                pltpu.VMEM((slots, 2, rows, order), f32),
                pltpu.VMEM((order, order), f32),
                pltpu.VMEM((2, order, order), f32),
                pltpu.VMEM((2, slots, 2, order, order), f32),
                pltpu.VMEM((slots, 2, rows, order), f32),
                pltpu.VMEM((3, order, order), bf16),
                pltpu.VMEM((3, order, order), bf16),
                pltpu.VMEM((6 * rows, order), bf16),
                pltpu.VMEM((slots, 2, 3 * rows, order), f32),
                pltpu.VMEM((slots, 2, 3, rows, order), f32),
                pltpu.VMEM(edge, f32),
                pltpu.VMEM(edge, f32),
                pltpu.VMEM(edge, f32),
                pltpu.VMEM(edge, f32),
                dma((2, 2, ring // 2, slots)),
                dma((2, 2, ring // 2, slots)),
                dma((2, 2)),
                dma((2, 2)),
                dma((2, slots)),
                dma((3,)),
            ],
            compiler_params=pltpu.CompilerParams(
                collective_id=0, has_side_effects=True, vmem_limit_bytes=50 * 1024 * 1024
            ),
        )(node_count, gamma, coeff, densities, hamiltonian, couplings)

    return jax.shard_map(
        on_device,
        mesh=mesh,
        in_specs=(P("hier", None, "col", None), P(), P(), P(), P(), P()),
        out_specs=P("hier", None, "col", None),
        check_vma=False,
    )
```

```python
import functools

import jax
import jax.numpy as jnp
from jax import lax
from jax.experimental import pallas as pl
from jax.experimental.pallas import tpu as pltpu
from jax.sharding import PartitionSpec as P

DEPTH2 = 2
MESH = pl.DeviceIdType.MESH
step_size = 0.2


def split(value):
    high = value.astype(jnp.bfloat16)
    low = (value - high.astype(jnp.float32)).astype(jnp.bfloat16)
    return high, low


def product(both, high, rhs_high, rhs_low):
    rows = high.shape[0]
    wide = jnp.dot(both, rhs_high, preferred_element_type=jnp.float32)
    rest = jnp.dot(high, rhs_low, preferred_element_type=jnp.float32)
    return wide[:rows] + (wide[rows:] + rest)


def kernel(
    shards,
    ring,
    counts,
    gamma,
    coeff,
    x_hbm,
    h_hbm,
    q_hbm,
    out_ref,
    x_ref,
    h_ref,
    q_ref,
    full,
    mid,
    right_high,
    right_low,
    left_both,
    lefts,
    rights,
    to_upper,
    to_lower,
    from_lower,
    from_upper,
    ring_send,
    ring_recv,
    hop_send,
    hop_recv,
    own_sem,
    load_sem,
):
    slots, _, rows, order = x_hbm.shape
    here = lax.axis_index("hier")
    me = lax.axis_index("col")
    reach = ring // 2
    right = (here, lax.rem(me + 1, ring))
    left = (here, lax.rem(me + ring - 1, ring))
    has_lower = here > 0
    has_upper = here < shards - 1

    loads = [
        pltpu.make_async_copy(source, place, load_sem.at[i])
        for i, (source, place) in enumerate(((x_hbm, x_ref), (h_hbm, h_ref), (q_hbm, q_ref)))
    ]
    for load in loads:
        load.start()

    barrier = pltpu.get_barrier_semaphore()
    for neighbour in (left, right):
        pl.semaphore_signal(barrier, inc=1, device_id=neighbour, device_id_type=MESH)

    @pl.when(has_lower)
    def _():
        pl.semaphore_signal(barrier, inc=1, device_id=(here - 1, me), device_id_type=MESH)

    @pl.when(has_upper)
    def _():
        pl.semaphore_signal(barrier, inc=1, device_id=(here + 1, me), device_id_type=MESH)

    pl.semaphore_wait(barrier, 2 + has_lower.astype(jnp.int32) + has_upper.astype(jnp.int32))

    def panel(origin):
        return pl.ds(pl.multiple_of(lax.rem(origin + ring, ring) * rows, rows), rows)

    def ring_copy(section, way, distance, s, origin):
        first, size = (way, 1) if 2 * distance == ring else (0, 2)
        parts = pl.ds(first, size)
        place = full.at[section, s, parts, panel(origin), :]
        if distance == 1:
            source = (x_hbm if section == 0 else mid).at[s, parts]
        else:
            source = place
        return pltpu.make_async_remote_copy(
            src_ref=source,
            dst_ref=place,
            send_sem=ring_send.at[section, way, distance - 1, s],
            recv_sem=ring_recv.at[section, way, distance - 1, s],
            device_id=right if way == 0 else left,
            device_id_type=MESH,
        )

    def sent(section, way, distance, s):
        origin = me - (distance - 1) if way == 0 else me + (distance - 1)
        return ring_copy(section, way, distance, s, origin)

    def arrived(section, way, distance, s):
        origin = me - distance if way == 0 else me + distance
        return ring_copy(section, way, distance, s, origin)

    def own_copy(section, s):
        source = (x_hbm if section == 0 else mid).at[s]
        return pltpu.make_async_copy(
            source, full.at[section, s, :, panel(me), :], own_sem.at[section, s]
        )

    def hop_copy(section, way):
        source, place = (to_upper, from_lower) if way == 0 else (to_lower, from_upper)
        return pltpu.make_async_remote_copy(
            src_ref=source.at[section],
            dst_ref=place.at[section],
            send_sem=hop_send.at[section, way],
            recv_sem=hop_recv.at[section, way],
            device_id=(here + 1, me) if way == 0 else (here - 1, me),
            device_id_type=MESH,
        )

    def start_slot(section, s):
        for way in range(2):
            sent(section, way, 1, s).start()
        own_copy(section, s).start()

    early, late = range(DEPTH2), range(DEPTH2, slots)
    for s in early:
        start_slot(0, s)

    for section in range(2):

        @pl.when(jnp.logical_not(has_lower))
        def _():
            from_lower[section] = jnp.zeros(from_lower.shape[1:], jnp.float32)

        @pl.when(jnp.logical_not(has_upper))
        def _():
            from_upper[section] = jnp.zeros(from_upper.shape[1:], jnp.float32)

    for load in loads:
        load.wait()
    mine = panel(me)
    for a in range(3):
        high, low = split(h_ref[...] if a == 0 else q_ref[a - 1])
        right_high[a], right_low[a] = high, low
        high, low = split(h_ref[mine, :] if a == 0 else q_ref[a - 1, mine, :])
        left_both[a * rows : (a + 1) * rows] = high
        left_both[(3 + a) * rows : (4 + a) * rows] = low

    offset = jnp.int32(0)
    total = jnp.int32(0)
    count = jnp.int32(0)
    for i in range(shards):
        held = counts[i]
        total = total + held
        offset = offset + jnp.where(here > i, held, 0)
        count = count + jnp.where(here == i, held, 0)
    live_total = total // DEPTH2 * DEPTH2

    def number(flag):
        return jnp.where(flag, jnp.float32(1), jnp.float32(0))

    def root(value):
        return jnp.sqrt(jnp.full((1, order), value, jnp.float32))

    def levels(q):
        node = offset + q
        level = (node + DEPTH2) // DEPTH2 - 1
        return level, node - level * DEPTH2, (node >= 0) & (node < live_total)

    alive, damping = [], []
    for s in range(slots):
        zeroth, first, inside = levels(s)
        alive.append(number(inside & (s < count)))
        damping.append(
            zeroth.astype(jnp.float32) * gamma[0] + first.astype(jnp.float32) * gamma[1]
        )
    edges = range(-DEPTH2, slots + DEPTH2)
    weights = {}
    for q in edges:
        zeroth, first, inside = levels(q)
        target = number(inside)
        base = jnp.maximum(zeroth, 0).astype(jnp.float32)
        above = first.astype(jnp.float32)
        if 0 <= q + DEPTH2 < slots:
            weights[q, "up0"] = root(base + 1.0) * (target * alive[q + DEPTH2])
        if 0 <= q - DEPTH2 < slots:
            weights[q, "down0"] = root(base) * (target * alive[q - DEPTH2])
        if 0 <= q + 1 < slots:
            ok = number(first + 1 < DEPTH2)
            weights[q, "up1"] = root(above + 1.0) * (target * alive[q + 1] * ok)
        if 0 <= q - 1 < slots:
            weights[q, "down1"] = root(above) * (target * alive[q - 1])

    def gathered(q):
        total_re = total_im = None

        def plus(total, term):
            return term if total is None else total + term

        for mode, stride in ((0, DEPTH2), (1, 1)):
            a = mode + 1
            for name, m in (("up", q + stride), ("down", q - stride)):
                if not 0 <= m < slots:
                    continue
                weight = weights[q, f"{name}{mode}"]
                left_re = lefts[m, 0, a * rows : (a + 1) * rows]
                left_im = lefts[m, 1, a * rows : (a + 1) * rows]
                right_re, right_im = rights[m, 0, a], rights[m, 1, a]
                if name == "up":
                    total_re = plus(total_re, weight * (left_re - right_re))
                    total_im = plus(total_im, weight * (left_im - right_im))
                else:
                    real = weight * coeff[mode, 0]
                    imag = weight * coeff[mode, 1]
                    total_re = plus(
                        total_re, real * (left_re - right_re) - imag * (left_im + right_im)
                    )
                    total_im = plus(
                        total_im, real * (left_im - right_im) + imag * (left_re + right_re)
                    )
        return total_re, total_im

    left_high = left_both[: 3 * rows]

    def right_products(section, chosen):
        state = x_ref if section == 0 else mid
        first, size = chosen[0], len(chosen)
        value = state[first : first + size].reshape(size * 2 * rows, order)
        high, low = split(value)
        both = jnp.concatenate([high, low], axis=0)
        for a in range(3):
            value = product(both, high, right_high[a], right_low[a])
            rights[first : first + size, :, a] = value.reshape(size, 2, rows, order)

    def forward(section, s):
        for distance in range(1, reach):
            for way in range(2):
                arrived(section, way, distance, s).wait_recv()
            for way in range(2):
                sent(section, way, distance + 1, s).start()

    def finish(section, s):
        own_copy(section, s).wait()
        for way in range(2):
            arrived(section, way, reach, s).wait_recv()
        for p in range(2):
            high, low = split(full[section, s, p])
            lefts[s, p] = product(left_both[...], left_high, high, low)

    def send_lower(section):
        for q in range(-DEPTH2, 0):
            value = gathered(q)
            for p in range(2):
                to_lower[section, q + DEPTH2, p] = value[p]

        @pl.when(has_lower)
        def _():
            hop_copy(section, 1).start()

    def send_upper(section, near):
        for j in range(DEPTH2):
            for p in range(2):
                value = None
                for q in range(DEPTH2 + j, slots + j + 1):
                    term = number(count + j == q) * near[q][p]
                    value = term if value is None else value + term
                to_upper[section, j, p] = value

        @pl.when(has_upper)
        def _():
            hop_copy(section, 0).start()

    def wait_upper(section):
        @pl.when(has_upper)
        def _():
            hop_copy(section, 1).wait_recv()

    def wait_lower(section):
        @pl.when(has_lower)
        def _():
            hop_copy(section, 0).wait_recv()

    def update(section, s, near):
        state = x_ref if section == 0 else mid
        parts = []
        for p in range(2):
            value = lefts[s, p, :rows] - rights[s, p, 0] + near[s][p]
            if s < DEPTH2:
                value = value + from_lower[section, s, p]
            for j in range(DEPTH2):
                value = value + number(s == count - DEPTH2 + j) * from_upper[section, j, p]
            parts.append(value)
        slope_re = (parts[1] - damping[s] * state[s, 0]) * alive[s]
        slope_im = (-parts[0] - damping[s] * state[s, 1]) * alive[s]
        place, length = (mid, 0.5 * step_size) if section == 0 else (out_ref, step_size)
        place[s, 0] = x_ref[s, 0] + length * slope_re
        place[s, 1] = x_ref[s, 1] + length * slope_im

    right_products(0, range(slots))
    for i, s in enumerate(early):
        forward(0, s)
        if DEPTH2 + i < slots:
            start_slot(0, DEPTH2 + i)
    for s in range(slots):
        if s >= 1 and s + DEPTH2 - 1 < slots:
            forward(0, s + DEPTH2 - 1)
        if s == DEPTH2:
            send_lower(0)
        finish(0, s)
    near = {q: gathered(q) for q in range(DEPTH2, slots + DEPTH2)}
    send_upper(0, near)
    wait_upper(0)
    for s in late:
        update(0, s, near)
        start_slot(1, s)
    near = {q: gathered(q) for q in early}
    for s in late:
        forward(1, s)
    wait_lower(0)
    for s in early:
        update(0, s, near)
        start_slot(1, s)
    right_products(1, early)
    right_products(1, late)
    for s in late:
        finish(1, s)
    for s in early:
        forward(1, s)
    for s in early:
        finish(1, s)
    send_lower(1)
    near = {q: gathered(q) for q in range(DEPTH2, slots + DEPTH2)}
    send_upper(1, near)
    near.update({q: gathered(q) for q in early})
    wait_upper(1)
    wait_lower(1)
    for s in range(slots):
        update(1, s, near)

    for section in range(2):
        for s in range(slots):
            for distance in range(1, reach + 1):
                for way in range(2):
                    sent(section, way, distance, s).wait_send()

        @pl.when(has_lower)
        def _():
            hop_copy(section, 1).wait_send()

        @pl.when(has_upper)
        def _():
            hop_copy(section, 0).wait_send()


def solution(mesh):
    shards, ring = mesh.shape["hier"], mesh.shape["col"]

    def on_device(densities, hamiltonian, couplings, gamma, coeff, node_count):
        slots, _, rows, order = densities.shape
        f32, bf16 = jnp.float32, jnp.bfloat16
        vmem = pl.BlockSpec(memory_space=pltpu.VMEM)
        smem = pl.BlockSpec(memory_space=pltpu.SMEM)
        edge = (2, DEPTH2, 2, rows, order)
        dma = pltpu.SemaphoreType.DMA
        return pl.pallas_call(
            functools.partial(kernel, shards, ring),
            out_shape=jax.ShapeDtypeStruct(densities.shape, f32),
            in_specs=[smem] * 3 + [pl.BlockSpec(memory_space=pltpu.HBM)] * 3,
            out_specs=vmem,
            scratch_shapes=[
                pltpu.VMEM((slots, 2, rows, order), f32),
                pltpu.VMEM((order, order), f32),
                pltpu.VMEM((2, order, order), f32),
                pltpu.VMEM((2, slots, 2, order, order), f32),
                pltpu.VMEM((slots, 2, rows, order), f32),
                pltpu.VMEM((3, order, order), bf16),
                pltpu.VMEM((3, order, order), bf16),
                pltpu.VMEM((6 * rows, order), bf16),
                pltpu.VMEM((slots, 2, 3 * rows, order), f32),
                pltpu.VMEM((slots, 2, 3, rows, order), f32),
                pltpu.VMEM(edge, f32),
                pltpu.VMEM(edge, f32),
                pltpu.VMEM(edge, f32),
                pltpu.VMEM(edge, f32),
                dma((2, 2, ring // 2, slots)),
                dma((2, 2, ring // 2, slots)),
                dma((2, 2)),
                dma((2, 2)),
                dma((2, slots)),
                dma((3,)),
            ],
            compiler_params=pltpu.CompilerParams(
                collective_id=0, has_side_effects=True, vmem_limit_bytes=67_043_328
            ),
        )(node_count, gamma, coeff, densities, hamiltonian, couplings)

    return jax.shard_map(
        on_device,
        mesh=mesh,
        in_specs=(P("hier", None, "col", None), P(), P(), P(), P(), P()),
        out_specs=P("hier", None, "col", None),
        check_vma=False,
    )
```
